32 devices in a mesh: dp: 2 (over core), context: 4 (over y, x), tensor: 4 (over z).
Axes of the slice: x: 2, y: 2, z: 4, core: 2. Of those that a mesh axis runs over, the one named last changes fastest.
Arguments:
- inputs: bfloat16 [3072, 1024], P(('dp', 'context')), may hold values from -6 to 6
- cotangent: bfloat16 [3072, 1024], P(('dp', 'context')), may hold values from -6 to 6
- initial_state: float32 [2, 4, 128, 256], P('dp', 'tensor'), may hold values from -6 to 6
- norm_one: float32 [1024], replicated, may hold values from 0.5 to 1.5
- query_weight: bfloat16 [1024, 512], P(('dp', 'context'), 'tensor'), may hold values from -0.1875 to 0.1875
- key_weight: bfloat16 [1024, 512], P(('dp', 'context'), 'tensor'), may hold values from -0.1875 to 0.1875
- value_weight: bfloat16 [1024, 1024], P(('dp', 'context'), 'tensor'), may hold values from -0.1875 to 0.1875
- outgate_weight: bfloat16 [1024, 1024], P(('dp', 'context'), 'tensor'), may hold values from -0.1875 to 0.1875
- output_weight: bfloat16 [1024, 1024], P(('dp', 'context'), 'tensor'), may hold values from -0.375 to 0.375
- lowrank_weight: bfloat16 [1024, 16], replicated, may hold values from -0.1875 to 0.1875
- rankup_weight: bfloat16 [16, 512], P(None, 'tensor'), may hold values from -1.5 to 1.5
- gate_bias: float32 [512], P('tensor'), may hold values from 0.5 to 8
- head_gain: float32 [256], replicated, may hold values from 0.5 to 1.5
- norm_two: float32 [1024], replicated, may hold values from 0.5 to 1.5
- gate_weight: bfloat16 [1024, 2816], P(('dp', 'context'), 'tensor'), may hold values from -0.1875 to 0.1875
- up_weight: bfloat16 [1024, 2816], P(('dp', 'context'), 'tensor'), may hold values from -0.1875 to 0.1875
- down_weight: bfloat16 [1024, 2816], P(('dp', 'context'), 'tensor'), may hold values from -0.21875 to 0.21875
Outputs:
- outputs: bfloat16 [3072, 1024], P(('dp', 'context'))
- grad_inputs: float32 [3072, 1024], P(('dp', 'context'))
- grad_norm_one: float32 [1024], replicated
- grad_query: float32 [1024, 512], P(('dp', 'context'), 'tensor')
- grad_key: float32 [1024, 512], P(('dp', 'context'), 'tensor')
- grad_value: float32 [1024, 1024], P(('dp', 'context'), 'tensor')
- grad_outgate: float32 [1024, 1024], P(('dp', 'context'), 'tensor')
- grad_output: float32 [1024, 1024], P(('dp', 'context'), 'tensor')
- grad_lowrank: float32 [1024, 16], replicated
- grad_rankup: float32 [16, 512], P(None, 'tensor')
- grad_bias: float32 [512], P('tensor')
- grad_head_gain: float32 [256], replicated
- grad_norm_two: float32 [1024], replicated
- grad_gate: float32 [1024, 2816], P(('dp', 'context'), 'tensor')
- grad_up: float32 [1024, 2816], P(('dp', 'context'), 'tensor')
- grad_down: float32 [1024, 2816], P(('dp', 'context'), 'tensor')
The draws below stay inside these ranges and needn't reach their ends.
All inputs are finite; a program needn't handle non-finite values.
Results may differ from the reference program's by a relative error of at most 0.011.
The reference program's roundings to bfloat16 on the way (of `normed_one`, `lowrank`, `gated`, `normed_two`, `product`, `low_logit` and `back_lowrank`) count: a program that leaves them out, or rounds other values in their place, can miss the bound.
Values may be sent and summed in bfloat16 or wider, within the bound.
No kernel may reach another device: no remote copies, remote signals or barrier semaphores. Data moves between devices by JAX's collectives and lax.ppermute only.
A program may use at most 128 MiB of HBM per device.

```python
import math
import jax
import jax.numpy as jnp
from jax import lax

D = 1024
HEADS = 4
DK = 512
DV = 1024
FF = 2816
RANK = 16
GROUP = 64
HEAD_K = 128
HEAD_V = 256
LENGTH = 1536
SEQUENCES = 2
TOKENS = 3072
N_DP = 2


def block_levels(key, shape, split, least, top_value):
    level, own = 1.0, jax.random.fold_in(key, 6)
    for position, shards_of in split:
        draws = jnp.exp(jax.random.uniform(jax.random.fold_in(own, position), (shards_of,), jnp.float32, least / len(split), top_value / len(split)))
        level = level * jnp.repeat(draws, shape[position] // shards_of).reshape([-1 if axis == position else 1 for axis in range(len(shape))])
    return level


def scatter_about(own_key, extent, width, most, cuts=(), kind=jnp.bfloat16):
    values = jax.random.normal(own_key, extent, jnp.float32) * width
    if len(cuts) > 0:
        values = block_levels(own_key, extent, cuts, -0.22, 0.18) * values
    return jnp.clip(values, min=-most, max=most).astype(kind)


def setup_inputs(seed: int = 0) -> dict:
    key_of = jax.random.split(jax.random.key(seed), 18)
    inputs = scatter_about(key_of[0], (TOKENS, D), 1.0, 6.0, ((0, 8),))
    cotangent = scatter_about(key_of[1], (TOKENS, D), 1.0, 6.0, ((0, 8),))
    initial_state = scatter_about(key_of[2], (SEQUENCES, HEADS, HEAD_K, HEAD_V), 1.0, 6.0, ((0, 2), (1, 4)), jnp.float32)
    norm_one = jnp.clip(1.0 + 0.1 * jax.random.normal(key_of[3], (D,), jnp.float32), 0.5, 1.5)
    query_weight = scatter_about(key_of[4], (D, DK), D ** -0.5, 0.1875, ((0, 8), (1, 4)))
    key_weight = scatter_about(key_of[5], (D, DK), D ** -0.5, 0.1875, ((0, 8), (1, 4)))
    value_weight = scatter_about(key_of[6], (D, DV), D ** -0.5, 0.1875, ((0, 8), (1, 4)))
    outgate_weight = scatter_about(key_of[7], (D, DV), D ** -0.5, 0.1875, ((0, 8), (1, 4)))
    output_weight = scatter_about(key_of[8], (D, DV), (DV // 4) ** -0.5, 0.375, ((0, 8), (1, 4)))
    lowrank_weight = scatter_about(key_of[9], (D, RANK), D ** -0.5, 0.1875)
    rankup_weight = scatter_about(key_of[10], (RANK, DK), RANK ** -0.5, 1.5, ((1, 4),))
    gate_bias = jnp.clip(jnp.exp(math.log(8.0) - 2.7725887 * jax.random.uniform(key_of[11], (DK,), jnp.float32) ** block_levels(key_of[11], (DK,), ((0, 4),), -0.2, 0.2)), 0.5, 8.0)
    head_gain = jnp.clip(1.0 + 0.1 * jax.random.normal(key_of[12], (HEAD_V,), jnp.float32), 0.5, 1.5)
    norm_two = jnp.clip(1.0 + 0.1 * jax.random.normal(key_of[13], (D,), jnp.float32), 0.5, 1.5)
    gate_weight = scatter_about(key_of[14], (D, FF), D ** -0.5, 0.1875, ((0, 8), (1, 4)))
    up_weight = scatter_about(key_of[15], (D, FF), D ** -0.5, 0.1875, ((0, 8), (1, 4)))
    down_weight = scatter_about(key_of[16], (D, FF), (FF // 4) ** -0.5, 0.21875, ((0, 8), (1, 4)))
    return {"inputs": inputs, "cotangent": cotangent, "initial_state": initial_state, "norm_one": norm_one, "query_weight": query_weight, "key_weight": key_weight, "value_weight": value_weight, "outgate_weight": outgate_weight, "output_weight": output_weight, "lowrank_weight": lowrank_weight, "rankup_weight": rankup_weight, "gate_bias": gate_bias, "head_gain": head_gain, "norm_two": norm_two, "gate_weight": gate_weight, "up_weight": up_weight, "down_weight": down_weight}


highest_precision = lax.Precision.HIGHEST
epsilon = 1e-06

def rms_scale(vectors, gain):
    inverse = lax.rsqrt(lax.optimization_barrier(jnp.mean(vectors * vectors, axis=-1, keepdims=True)) + epsilon)
    return vectors * inverse * gain

def rms_back(vectors, gain, upstream):
    inverse = lax.rsqrt(lax.optimization_barrier(jnp.mean(vectors * vectors, axis=-1, keepdims=True)) + epsilon)
    normal_part = vectors * inverse
    scaled_up = upstream * gain
    back_vectors = inverse * (scaled_up - normal_part * lax.optimization_barrier(jnp.mean(scaled_up * normal_part, axis=-1, keepdims=True)))
    return (back_vectors, upstream * normal_part)

def project(left, weight):
    return jnp.dot(left, weight, preferred_element_type=jnp.float32)

def project_back(left, weight):
    return lax.dot_general(left, weight, (((1,), (1,)), ((), ())), preferred_element_type=jnp.float32)

def weight_grad(left, right):
    return lax.dot_general(left, right, (((0,), (0,)), ((), ())), preferred_element_type=jnp.float32)

def swish_slope(preact):
    sigma = jax.nn.sigmoid(preact)
    return sigma * (1.0 + preact * (1.0 - sigma))

def gla_core(query, keys, values, log_decay, start_state):
    length = keys.shape[0]
    blocks = length // GROUP
    causal = jnp.tril(jnp.ones((GROUP, GROUP), jnp.float32))

    def advance(state, pieces):
        query_blk, key_blk, value_blk, decay_blk = pieces
        running = jnp.cumsum(decay_blk, axis=0)
        ending = running[-1]
        query_up = query_blk * jnp.exp(running)
        key_down = key_blk * jnp.exp(-running)
        scores = jnp.dot(query_up, key_down.T, precision=highest_precision) * causal
        within = jnp.dot(scores, value_blk, precision=highest_precision) + jnp.dot(query_up, state, precision=highest_precision)
        key_tail = key_blk * jnp.exp(ending - running)
        state = jnp.exp(ending)[:, None] * state + jnp.dot(key_tail.T, value_blk, precision=highest_precision)
        return (state, within)
    final_state, pieces_out = lax.scan(advance, start_state, (query.reshape(blocks, GROUP, -1), keys.reshape(blocks, GROUP, -1), values.reshape(blocks, GROUP, -1), log_decay.reshape(blocks, GROUP, -1)))
    return (pieces_out.reshape(length, values.shape[1]), final_state)

def core_heads(query, keys, values, log_decay, start_states):
    return jax.vmap(gla_core, in_axes=(1, 1, 1, 1, 0), out_axes=(1, 0))(query, keys, values, log_decay, start_states)

def gate_norm(attention_result, outgate, head_gain):
    return rms_scale(attention_result, head_gain) * outgate * jax.nn.sigmoid(outgate)

def reference(inputs, cotangent, initial_state, norm_one, query_weight, key_weight, value_weight, outgate_weight, output_weight, lowrank_weight, rankup_weight, gate_bias, head_gain, norm_two, gate_weight, up_weight, down_weight):
    scale = HEAD_K ** (-0.5)

    def sequence_pass(totals, batch):
        seq_inputs, seq_cotangent, seq_start = batch

        def core_output(query, keys, values, log_decay):
            return core_heads(query, keys, values, log_decay, seq_start)[0]
        stream = seq_inputs.astype(jnp.float32)
        normed_one = rms_scale(stream, norm_one).astype(jnp.bfloat16)
        query = (project(normed_one, query_weight) * scale).reshape(LENGTH, HEADS, HEAD_K)
        keys = project(normed_one, key_weight).reshape(LENGTH, HEADS, HEAD_K)
        values = project(normed_one, value_weight).reshape(LENGTH, HEADS, HEAD_V)
        outgate = project(normed_one, outgate_weight).reshape(LENGTH, HEADS, HEAD_V)
        lowrank = project(normed_one, lowrank_weight).astype(jnp.bfloat16)
        gate_logit = project(lowrank, rankup_weight) + gate_bias
        log_decay = (jax.nn.log_sigmoid(gate_logit) / 16.0).reshape(LENGTH, HEADS, HEAD_K)
        attention_result = core_output(query, keys, values, log_decay)
        gated = gate_norm(attention_result, outgate, head_gain).reshape(LENGTH, DV).astype(jnp.bfloat16)
        hidden = stream + project_back(gated, output_weight)
        normed_two = rms_scale(hidden, norm_two).astype(jnp.bfloat16)
        gate_input = project(normed_two, gate_weight)
        up_input = project(normed_two, up_weight)
        product = (jax.nn.silu(gate_input) * up_input).astype(jnp.bfloat16)
        result = hidden + project_back(product, down_weight)
        back_product = project(seq_cotangent, down_weight)
        grad_down = weight_grad(seq_cotangent, product)
        back_up = (back_product * jax.nn.silu(gate_input)).astype(jnp.bfloat16)
        back_gate = (back_product * up_input * swish_slope(gate_input)).astype(jnp.bfloat16)
        grad_gate = weight_grad(normed_two, back_gate)
        grad_up = weight_grad(normed_two, back_up)
        back_normed_two = project_back(back_gate, gate_weight) + project_back(back_up, up_weight)
        back_hidden_norm, gain_two_rows = rms_back(hidden, norm_two, back_normed_two)
        back_hidden = seq_cotangent.astype(jnp.float32) + back_hidden_norm
        back_low = back_hidden.astype(jnp.bfloat16)
        back_gated = project(back_low, output_weight)
        grad_output = weight_grad(back_low, gated)
        ignored, gate_pull = jax.vjp(gate_norm, attention_result, outgate, head_gain)
        attention_backward_pass, back_outgate, grad_head = gate_pull(back_gated.reshape(LENGTH, HEADS, HEAD_V))
        ignored, core_pull = jax.vjp(core_output, query, keys, values, log_decay)
        back_query, back_keys, back_values, back_decay = core_pull(attention_backward_pass)
        low_query = (back_query.reshape(LENGTH, DK) * scale).astype(jnp.bfloat16)
        low_keys = back_keys.reshape(LENGTH, DK).astype(jnp.bfloat16)
        low_values = back_values.reshape(LENGTH, DV).astype(jnp.bfloat16)
        low_outgate = back_outgate.reshape(LENGTH, DV).astype(jnp.bfloat16)
        back_logit = back_decay.reshape(LENGTH, DK) * jax.nn.sigmoid(-gate_logit) / 16.0
        grad_bias = lax.optimization_barrier(jnp.sum(back_logit, axis=0))
        low_logit = back_logit.astype(jnp.bfloat16)
        grad_rankup = weight_grad(lowrank, low_logit)
        back_lowrank = jnp.einsum('shk,rhk->shr', low_logit.reshape(LENGTH, HEADS, HEAD_K).astype(jnp.float32), rankup_weight.reshape(RANK, HEADS, HEAD_K).astype(jnp.float32)).astype(jnp.bfloat16)
        grad_lowrank = jnp.einsum('sd,shr->dr', normed_one.astype(jnp.float32), back_lowrank.astype(jnp.float32))
        grad_query = weight_grad(normed_one, low_query)
        grad_key = weight_grad(normed_one, low_keys)
        grad_value = weight_grad(normed_one, low_values)
        grad_outgate = weight_grad(normed_one, low_outgate)
        back_normed_one = project_back(low_query, query_weight) + project_back(low_keys, key_weight) + project_back(low_values, value_weight) + project_back(low_outgate, outgate_weight) + jnp.einsum('shr,dr->sd', back_lowrank.astype(jnp.float32), lowrank_weight.astype(jnp.float32))
        back_stream, gain_one_rows = rms_back(stream, norm_one, back_normed_one)
        grad_stream = back_hidden + back_stream
        terms = (lax.optimization_barrier(jnp.sum(gain_one_rows, axis=0)), grad_query, grad_key, grad_value, grad_outgate, grad_output, grad_lowrank, grad_rankup, grad_bias, grad_head, lax.optimization_barrier(jnp.sum(gain_two_rows, axis=0)), grad_gate, grad_up, grad_down)
        totals = tuple((total + term for total, term in zip(totals, terms)))
        return (totals, (result.astype(jnp.bfloat16), grad_stream))
    zero_totals = (jnp.zeros((D,), jnp.float32), jnp.zeros((D, DK), jnp.float32), jnp.zeros((D, DK), jnp.float32), jnp.zeros((D, DV), jnp.float32), jnp.zeros((D, DV), jnp.float32), jnp.zeros((D, DV), jnp.float32), jnp.zeros((D, RANK), jnp.float32), jnp.zeros((RANK, DK), jnp.float32), jnp.zeros((DK,), jnp.float32), jnp.zeros((HEAD_V,), jnp.float32), jnp.zeros((D,), jnp.float32), jnp.zeros((D, FF), jnp.float32), jnp.zeros((D, FF), jnp.float32), jnp.zeros((D, FF), jnp.float32))
    totals, (outputs, grad_inputs) = lax.scan(sequence_pass, zero_totals, (inputs.reshape(N_DP, LENGTH, D), cotangent.reshape(N_DP, LENGTH, D), initial_state))
    return (outputs.reshape(TOKENS, D), grad_inputs.reshape(TOKENS, D), totals[0], totals[1], totals[2], totals[3], totals[4], totals[5], totals[6], totals[7], totals[8], totals[9], totals[10], totals[11], totals[12], totals[13])
```

```python
import functools

import jax
import jax.numpy as jnp
from jax import lax
from jax.experimental import pallas as pl
from jax.experimental.pallas import tpu as pltpu
from jax.sharding import PartitionSpec as P

GROUP = 64
HEAD_K = 128
HEAD_V = 256
epsilon = 1e-06
bf16 = jnp.bfloat16
f32 = jnp.float32


def power_of_two(count):
    return count & (count - 1) == 0


def exchange(value, axis, mask):
    count = lax.axis_size(axis)
    return lax.ppermute(value, axis, [(i, i ^ mask) for i in range(count)])


def shifted(value, axis, step):
    count = lax.axis_size(axis)
    pairs = [(i, i + step) for i in range(count) if 0 <= i + step < count]
    return lax.ppermute(value, axis, pairs)


def place(pieces, order, axis):
    size = pieces[0].shape[axis]
    shape = list(pieces[0].shape)
    shape[axis] = size * len(pieces)
    whole = jnp.zeros(shape, pieces[0].dtype)
    for piece, block in zip(pieces, order):
        whole = lax.dynamic_update_slice_in_dim(whole, piece, block * size, axis)
    return whole


def gather_rows(shard, axis):
    across, along = lax.axis_size("dp"), lax.axis_size("context")
    if across != 2 or not power_of_two(along):
        return lax.all_gather(shard, ("dp", "context"), axis=axis, tiled=True)
    core, mine = lax.axis_index("dp"), lax.axis_index("context")
    near = [shard] + [exchange(shard, "context", mask) for mask in range(1, along)]
    far = [exchange(piece, "dp", 1) for piece in near]
    order = [core * along + (mine ^ mask) for mask in range(along)]
    order += [(1 - core) * along + (mine ^ mask) for mask in range(along)]
    return place(near + far, order, axis)


def scatter_rows(whole, axis):
    across, along = lax.axis_size("dp"), lax.axis_size("context")
    if across != 2 or not power_of_two(along):
        return lax.psum_scatter(
            whole.astype(f32), ("dp", "context"), scatter_dimension=axis, tiled=True
        )
    core, mine = lax.axis_index("dp"), lax.axis_index("context")
    half = whole.shape[axis] // 2
    keep = lax.dynamic_slice_in_dim(whole, core * half, half, axis)
    give = lax.dynamic_slice_in_dim(whole, (1 - core) * half, half, axis)
    both = (keep.astype(f32) + exchange(give, "dp", 1).astype(f32)).astype(bf16)
    part = half // along
    total = lax.dynamic_slice_in_dim(both, mine * part, part, axis).astype(f32)
    for mask in range(1, along):
        piece = lax.dynamic_slice_in_dim(both, (mine ^ mask) * part, part, axis)
        total = total + exchange(piece, "context", mask).astype(f32)
    return total


def scatter_tokens(partial):
    count, mine = lax.axis_size("tensor"), lax.axis_index("tensor")
    if not power_of_two(count):
        return lax.psum_scatter(partial, "tensor", scatter_dimension=0, tiled=True)
    part = partial.shape[0] // count
    total = lax.dynamic_slice_in_dim(partial, mine * part, part, 0).astype(f32)
    for mask in range(1, count):
        piece = lax.dynamic_slice_in_dim(partial, (mine ^ mask) * part, part, 0)
        total = total + exchange(piece.astype(bf16), "tensor", mask).astype(f32)
    return total


def gather_tokens(part):
    count, mine = lax.axis_size("tensor"), lax.axis_index("tensor")
    if not power_of_two(count):
        return lax.all_gather(part, "tensor", axis=0, tiled=True)
    pieces = [part] + [exchange(part, "tensor", mask) for mask in range(1, count)]
    return place(pieces, [mine ^ mask for mask in range(count)], 0)


def sum_over(value, axes):
    for axis in axes:
        count = lax.axis_size(axis)
        if power_of_two(count):
            mask = 1
            while mask < count:
                value = value + exchange(value, axis, mask)
                mask *= 2
        else:
            value = lax.psum(value, axis)
    return value


def exact(left, right, contract):
    return lax.dot_general(
        left,
        right,
        ((contract[0], contract[1]), ((), ())),
        precision=lax.Precision.HIGHEST,
        preferred_element_type=f32,
    )


def nn(left, right):
    return exact(left, right, ((1,), (0,)))


def nt(left, right):
    return exact(left, right, ((1,), (1,)))


def tn(left, right):
    return exact(left, right, ((0,), (0,)))


def lower_ones(size, strict=False):
    row = lax.broadcasted_iota(jnp.int32, (size, size), 0)
    col = lax.broadcasted_iota(jnp.int32, (size, size), 1)
    return row >= col


def state_kernel(block, decay_ref, key_ref, value_ref, run_ref, start_ref, state_ref, pack_ref):
    rows = decay_ref.shape[0]
    ones = lower_ones(block).astype(f32)
    state = jnp.zeros((HEAD_V, HEAD_K), f32)
    start = jnp.zeros((1, HEAD_K), f32)
    for b in range(rows // block):
        cut = slice(b * block, (b + 1) * block)
        run = nn(ones, decay_ref[cut, :])
        end = run[block - 1 : block, :]
        run_ref[cut, :] = run
        start_ref[b : b + 1, :] = start
        state_ref[b] = state
        tail = key_ref[cut, :] * jnp.exp(end - run)
        state = jnp.exp(end) * state + tn(value_ref[cut, :], tail)
        start = start + end
    pack_ref[0:HEAD_V, :] = state
    pack_ref[HEAD_V : HEAD_V + 8, :] = jnp.broadcast_to(start, (8, HEAD_K))


def inner_kernel(block, query_ref, key_ref, value_ref, run_ref, state_ref, out_ref):
    rows = query_ref.shape[0]
    causal = lower_ones(block)
    for b in range(rows // block):
        cut = slice(b * block, (b + 1) * block)
        run = run_ref[cut, :]
        mid = run[block // 2 - 1 : block // 2, :]
        query, keys, values = query_ref[cut, :], key_ref[cut, :], value_ref[cut, :]
        scores = nt(query * jnp.exp(run - mid), keys * jnp.exp(mid - run))
        scores = jnp.where(causal, scores, 0.0)
        out_ref[cut, :] = nn(scores, values) + nt(query * jnp.exp(run), state_ref[b])


def chained(pack_refs):
    state = jnp.zeros((HEAD_V, HEAD_K), f32)
    total = jnp.zeros((1, HEAD_K), f32)
    for ref in pack_refs:
        state = state + jnp.exp(total) * ref[0:HEAD_V, :]
        total = total + ref[HEAD_V : HEAD_V + 1, :]
    return state, total


def gate_kernel(block, count, *refs):
    (local_ref, query_ref, run_ref, start_ref, initial_ref, outgate_ref, gain_ref) = refs[:7]
    packs = refs[7 : 7 + count]
    out_ref, gated_ref, incoming_ref = refs[7 + count :]
    state, total = chained(packs)
    state = state + jnp.exp(total) * initial_ref[...]
    incoming_ref[...] = state
    rows = query_ref.shape[0]
    gain = gain_ref[...]
    for b in range(rows // block):
        cut = slice(b * block, (b + 1) * block)
        run = run_ref[cut, :] + start_ref[b : b + 1, :]
        result = local_ref[cut, :] + nt(query_ref[cut, :] * jnp.exp(run), state)
        out_ref[cut, :] = result
        inverse = lax.rsqrt(jnp.mean(result * result, axis=-1, keepdims=True) + epsilon)
        outgate = outgate_ref[cut, :]
        gated = result * inverse * gain * outgate * jax.nn.sigmoid(outgate)
        gated_ref[cut, :] = gated.astype(bf16)


def ungate_kernel(block, *refs):
    (up_ref, out_ref, outgate_ref, gain_ref, query_ref, run_ref, start_ref, total_ref) = refs[:8]
    back_ref, low_ref, head_ref, pack_ref = refs[8:]
    rows = query_ref.shape[0]
    gain = gain_ref[...]
    state = jnp.zeros((HEAD_V, HEAD_K), f32)
    head = jnp.zeros((1, HEAD_V), f32)
    for b in range(rows // block):
        cut = slice(b * block, (b + 1) * block)
        result, outgate, upstream = out_ref[cut, :], outgate_ref[cut, :], up_ref[cut, :]
        inverse = lax.rsqrt(jnp.mean(result * result, axis=-1, keepdims=True) + epsilon)
        normal = result * inverse
        sigma = jax.nn.sigmoid(outgate)
        low_ref[cut, :] = (
            upstream * normal * gain * (sigma * (1.0 + outgate * (1.0 - sigma)))
        ).astype(bf16)
        upstream = upstream * (outgate * sigma)
        head = head + jnp.sum(upstream * normal, axis=0, keepdims=True)
        upstream = upstream * gain
        back = inverse * (
            upstream - normal * jnp.mean(upstream * normal, axis=-1, keepdims=True)
        )
        back_ref[cut, :] = back
        run = run_ref[cut, :] + start_ref[b : b + 1, :]
        state = state + tn(back, query_ref[cut, :] * jnp.exp(run))
    head_ref[...] = jnp.broadcast_to(head, (8, HEAD_V))
    pack_ref[0:HEAD_V, :] = state
    pack_ref[HEAD_V : HEAD_V + 8, :] = total_ref[...]


def uninner_kernel(block, *refs):
    (query_ref, key_ref, value_ref, run_ref, start_ref, state_ref, incoming_ref, back_ref) = refs[:8]
    dquery_ref, dkey_ref, dvalue_ref = refs[8:]
    rows = query_ref.shape[0]
    causal = lower_ones(block)
    incoming = incoming_ref[...]
    later = jnp.zeros((HEAD_V, HEAD_K), f32)
    for b in reversed(range(rows // block)):
        cut = slice(b * block, (b + 1) * block)
        run = run_ref[cut, :]
        mid = run[block // 2 - 1 : block // 2, :]
        end = run[block - 1 : block, :]
        query, keys, values = query_ref[cut, :], key_ref[cut, :], value_ref[cut, :]
        back = back_ref[cut, :]
        rise, fall = jnp.exp(run - mid), jnp.exp(mid - run)
        decay, tail = jnp.exp(run), jnp.exp(end - run)
        query_up, key_down, key_tail = query * rise, keys * fall, keys * tail
        scores = jnp.where(causal, nt(query_up, key_down), 0.0)
        back_scores = jnp.where(causal, nt(back, values), 0.0)
        state = state_ref[b] + jnp.exp(start_ref[b : b + 1, :]) * incoming
        dquery_ref[cut, :] = rise * nn(back_scores, key_down) + decay * nn(back, state)
        dkey_ref[cut, :] = fall * tn(back_scores, query_up) + tail * nn(values, later)
        dvalue_ref[cut, :] = tn(scores, back) + nt(key_tail, later)
        later = jnp.exp(end) * later + tn(back, query * decay)


def finish_kernel(block, count, scale, *refs):
    (query_ref, key_ref, value_ref, run_ref, start_ref, pack_ref, incoming_ref) = refs[:7]
    (dquery_ref, dkey_ref, dvalue_ref, logit_ref) = refs[7:11]
    packs = refs[11 : 11 + count]
    lowq_ref, lowk_ref, lowv_ref, lowl_ref, bias_ref = refs[11 + count :]
    rows = query_ref.shape[0]
    suffix, _ = chained(packs)
    total = pack_ref[HEAD_V : HEAD_V + 1, :]
    outgoing = pack_ref[0:HEAD_V, :] + jnp.exp(total) * incoming_ref[...]
    carry = jnp.sum(outgoing * suffix, axis=0, keepdims=True)
    ones = lower_ones(block).astype(f32)
    bias = jnp.zeros((1, HEAD_K), f32)
    for b in reversed(range(rows // block)):
        cut = slice(b * block, (b + 1) * block)
        tail = jnp.exp(total - (run_ref[cut, :] + start_ref[b : b + 1, :]))
        keys = key_ref[cut, :]
        dquery = dquery_ref[cut, :]
        dkey = dkey_ref[cut, :] + tail * nn(value_ref[cut, :], suffix)
        lowv_ref[cut, :] = (dvalue_ref[cut, :] + nt(keys * tail, suffix)).astype(bf16)
        lowq_ref[cut, :] = (dquery * scale).astype(bf16)
        lowk_ref[cut, :] = dkey.astype(bf16)
        change = query_ref[cut, :] * dquery - keys * dkey
        back = tn(ones, change) + carry
        carry = back[0:1, :]
        back = back * jax.nn.sigmoid(-logit_ref[cut, :]) / 16.0
        bias = bias + jnp.sum(back, axis=0, keepdims=True)
        lowl_ref[cut, :] = back.astype(bf16)
    bias_ref[...] = jnp.broadcast_to(bias, (8, HEAD_K))


def rms_inverse(vectors):
    return lax.rsqrt(jnp.mean(vectors * vectors, axis=-1, keepdims=True) + epsilon)


def rms_back(vectors, gain, upstream):
    inverse = rms_inverse(vectors)
    normal_part = vectors * inverse
    scaled_up = upstream * gain
    back_vectors = inverse * (
        scaled_up - normal_part * jnp.mean(scaled_up * normal_part, axis=-1, keepdims=True)
    )
    return (back_vectors, upstream * normal_part)


def project(left, weight):
    return jnp.dot(left, weight, preferred_element_type=f32)


def project_back(left, weight):
    return lax.dot_general(left, weight, (((1,), (1,)), ((), ())), preferred_element_type=f32)


def weight_grad(left, right):
    return lax.dot_general(left, right, (((0,), (0,)), ((), ())), preferred_element_type=f32)


def local(
    inputs,
    cotangent,
    initial_state,
    norm_one,
    query_weight,
    key_weight,
    value_weight,
    outgate_weight,
    output_weight,
    lowrank_weight,
    rankup_weight,
    gate_bias,
    head_gain,
    norm_two,
    gate_weight,
    up_weight,
    down_weight,
):
    rows, width = inputs.shape
    heads = query_weight.shape[1] // HEAD_K
    wide_k, wide_v = heads * HEAD_K, heads * HEAD_V
    rank = lowrank_weight.shape[1]
    scale = HEAD_K ** (-0.5)
    block = 2 * GROUP if rows % (2 * GROUP) == 0 else GROUP
    blocks = rows // block
    padded = -(-blocks // 8) * 8
    spans = lax.axis_size("context")
    others = spans - 1
    tall = HEAD_V + 8
    mine = lax.axis_index("tensor")
    part = rows // lax.axis_size("tensor")

    def span(columns, first=0):
        return pl.BlockSpec((rows, columns), lambda h, first=first: (0, first + h))

    def per_head(*shape):
        return pl.BlockSpec((None, *shape), lambda h: (h,) + (0,) * len(shape))

    def shape_of(*shape, kind=f32):
        return jax.ShapeDtypeStruct(shape, kind)

    gain_spec = pl.BlockSpec((1, HEAD_V), lambda h: (0, 0))
    run_spec, start_spec = span(HEAD_K), per_head(padded, HEAD_K)
    state_spec, pack_spec = per_head(blocks, HEAD_V, HEAD_K), per_head(tall, HEAD_K)
    incoming_spec = per_head(HEAD_V, HEAD_K)
    q_spec, k_spec = span(HEAD_K), span(HEAD_K, heads)
    v_spec, g_spec = span(HEAD_V, heads), span(HEAD_V, 2 * heads)

    attention_shard = jnp.concatenate(
        [query_weight, key_weight, value_weight, outgate_weight, output_weight], axis=1
    )
    attention_weight = gather_rows(attention_shard, 0)
    mixing = attention_weight[:, : 2 * wide_k + 2 * wide_v]
    output_full = attention_weight[:, 2 * wide_k + 2 * wide_v :]

    stream = inputs.astype(f32)
    stream_inverse = rms_inverse(stream)
    normed_one = (stream * stream_inverse * norm_one).astype(bf16)
    lowrank = project(normed_one, lowrank_weight).astype(bf16)
    gate_logit = project(lowrank, rankup_weight) + gate_bias
    log_decay = jax.nn.log_sigmoid(gate_logit) / 16.0
    start_states = jnp.swapaxes(initial_state[0], 1, 2)
    gain_row = head_gain.reshape(1, HEAD_V)

    column_scale = jnp.concatenate(
        [jnp.full((wide_k,), scale, f32), jnp.ones((wide_k + 2 * wide_v,), f32)]
    )
    mixed = project(normed_one, mixing) * column_scale

    ffn_shard = jnp.stack([gate_weight, up_weight, down_weight])
    ffn_weight = gather_rows(ffn_shard, 1)
    gate_full, up_full, down_full = ffn_weight[0], ffn_weight[1], ffn_weight[2]

    run, start, states, pack = pl.pallas_call(
        functools.partial(state_kernel, block),
        grid=(heads,),
        in_specs=[run_spec, k_spec, v_spec],
        out_specs=[run_spec, start_spec, state_spec, pack_spec],
        out_shape=[
            shape_of(rows, wide_k),
            shape_of(heads, padded, HEAD_K),
            shape_of(heads, blocks, HEAD_V, HEAD_K),
            shape_of(heads, tall, HEAD_K),
        ],
        name="span_state",
    )(log_decay, mixed, mixed)
    before = [shifted(pack, "context", step) for step in range(1, spans)]
    local_out = pl.pallas_call(
        functools.partial(inner_kernel, block),
        grid=(heads,),
        in_specs=[q_spec, k_spec, v_spec, run_spec, state_spec],
        out_specs=span(HEAD_V),
        out_shape=shape_of(rows, wide_v),
        name="span_inner",
    )(mixed, mixed, mixed, run, states)
    attention, gated, incoming = pl.pallas_call(
        functools.partial(gate_kernel, block, others),
        grid=(heads,),
        in_specs=[span(HEAD_V), q_spec, run_spec, start_spec, incoming_spec, g_spec, gain_spec]
        + [pack_spec] * others,
        out_specs=[span(HEAD_V), span(HEAD_V), incoming_spec],
        out_shape=[
            shape_of(rows, wide_v),
            shape_of(rows, wide_v, kind=bf16),
            shape_of(heads, HEAD_V, HEAD_K),
        ],
        name="span_gate",
    )(local_out, mixed, run, start, start_states, mixed, gain_row, *before)

    stream_part = lax.dynamic_slice_in_dim(stream, mine * part, part, 0)
    cotangent_part = lax.dynamic_slice_in_dim(cotangent, mine * part, part, 0).astype(f32)
    hidden = stream_part + scatter_tokens(project_back(gated, output_full))
    normed_two = gather_tokens((hidden * rms_inverse(hidden) * norm_two).astype(bf16))
    back_product = project(cotangent, down_full)
    gate_input = project(normed_two, gate_full)
    up_input = project(normed_two, up_full)
    sigma = jax.nn.sigmoid(gate_input)
    swish = gate_input * sigma
    product = (swish * up_input).astype(bf16)
    back_up = (back_product * swish).astype(bf16)
    back_gate = (
        back_product * up_input * (sigma * (1.0 + gate_input * (1.0 - sigma)))
    ).astype(bf16)
    back_normed_two = scatter_tokens(
        project_back(back_gate, gate_full) + project_back(back_up, up_full)
    )
    back_hidden_norm, gain_two_rows = rms_back(hidden, norm_two, back_normed_two)
    back_hidden = cotangent_part + back_hidden_norm
    back_low = gather_tokens(back_hidden.astype(bf16))
    gain_two = jnp.sum(gain_two_rows, axis=0)

    grad_ffn = jnp.stack(
        [
            weight_grad(normed_two, back_gate).astype(bf16),
            weight_grad(normed_two, back_up).astype(bf16),
            weight_grad(cotangent, product).astype(bf16),
        ]
    )
    ffn_out = scatter_rows(grad_ffn, 1)

    product_later, back_low = lax.optimization_barrier((product, back_low))
    result = hidden + scatter_tokens(project_back(product_later, down_full))
    outputs = gather_tokens(result.astype(bf16))

    back_gated = project(back_low, output_full)
    back_attention, low_outgate, head_rows, back_pack = pl.pallas_call(
        functools.partial(ungate_kernel, block),
        grid=(heads,),
        in_specs=[span(HEAD_V), span(HEAD_V), g_spec, gain_spec, q_spec, run_spec, start_spec]
        + [pl.BlockSpec((None, 8, HEAD_K), lambda h: (h, HEAD_V // 8, 0))],
        out_specs=[span(HEAD_V), span(HEAD_V), per_head(8, HEAD_V), pack_spec],
        out_shape=[
            shape_of(rows, wide_v),
            shape_of(rows, wide_v, kind=bf16),
            shape_of(heads, 8, HEAD_V),
            shape_of(heads, tall, HEAD_K),
        ],
        name="span_ungate",
    )(back_gated, attention, mixed, gain_row, mixed, run, start, pack)
    after = [shifted(back_pack, "context", -step) for step in range(1, spans)]
    dquery, dkey, dvalue = pl.pallas_call(
        functools.partial(uninner_kernel, block),
        grid=(heads,),
        in_specs=[q_spec, k_spec, v_spec, run_spec, start_spec, state_spec, incoming_spec]
        + [span(HEAD_V)],
        out_specs=[span(HEAD_K), span(HEAD_K), span(HEAD_V)],
        out_shape=[shape_of(rows, wide_k), shape_of(rows, wide_k), shape_of(rows, wide_v)],
        name="span_uninner",
    )(mixed, mixed, mixed, run, start, states, incoming, back_attention)
    low_query, low_keys, low_values, low_logit, bias_rows = pl.pallas_call(
        functools.partial(finish_kernel, block, others, scale),
        grid=(heads,),
        in_specs=[q_spec, k_spec, v_spec, run_spec, start_spec, pack_spec, incoming_spec]
        + [span(HEAD_K), span(HEAD_K), span(HEAD_V), span(HEAD_K)]
        + [pack_spec] * others,
        out_specs=[span(HEAD_K), span(HEAD_K), span(HEAD_V), span(HEAD_K), per_head(8, HEAD_K)],
        out_shape=[
            shape_of(rows, wide_k, kind=bf16),
            shape_of(rows, wide_k, kind=bf16),
            shape_of(rows, wide_v, kind=bf16),
            shape_of(rows, wide_k, kind=bf16),
            shape_of(heads, 8, HEAD_K),
        ],
        name="span_finish",
    )(mixed, mixed, mixed, run, start, pack, incoming, dquery, dkey, dvalue, gate_logit, *after)

    low_mixed = jnp.concatenate([low_query, low_keys, low_values, low_outgate], axis=1)
    partial_one = project_back(low_mixed, mixing)
    grad_lowrank = jnp.zeros((rank, width), f32)
    for h in range(heads):
        cut = slice(h * HEAD_K, (h + 1) * HEAD_K)
        back_lowrank = project_back(low_logit[:, cut], rankup_weight[:, cut]).astype(bf16)
        partial_one = partial_one + project_back(back_lowrank, lowrank_weight)
        grad_lowrank = grad_lowrank + weight_grad(back_lowrank, normed_one)
    grad_rankup = weight_grad(lowrank, low_logit)
    back_normed_one = scatter_tokens(partial_one)
    gain_one = jnp.sum(partial_one * (stream * stream_inverse), axis=0)
    back_stream, _ = rms_back(stream_part, norm_one, back_normed_one)
    grad_inputs = gather_tokens((back_hidden + back_stream).astype(bf16)).astype(f32)

    grad_mixed = jnp.concatenate(
        [
            weight_grad(normed_one, low_mixed).astype(bf16),
            weight_grad(back_low, gated).astype(bf16),
        ],
        axis=1,
    )
    mixed_out = scatter_rows(grad_mixed, 0)

    grad_head = jnp.sum(head_rows[:, 0, :], axis=0)
    small = jnp.concatenate(
        [gain_one[None], gain_two[None], grad_lowrank]
        + [jnp.pad(grad_head, (0, width - HEAD_V))[None]]
    )
    slim = jnp.concatenate([grad_rankup, bias_rows[:, 0, :].reshape(1, wide_k)])
    flat = jnp.concatenate([small.reshape(-1), slim.reshape(-1)])
    rest = -flat.shape[0] % width
    flat = jnp.pad(flat, (0, rest)).reshape(-1, width)
    flat = sum_over(flat, ("dp", "context"))
    small = sum_over(flat[: rank + 3], ("tensor",))
    slim = flat[rank + 3 :].reshape(-1)[: (rank + 1) * wide_k].reshape(rank + 1, wide_k)

    a, b, c = wide_k, 2 * wide_k, 2 * wide_k + wide_v
    d = c + wide_v
    return (
        outputs,
        grad_inputs,
        small[0],
        mixed_out[:, :a],
        mixed_out[:, a:b],
        mixed_out[:, b:c],
        mixed_out[:, c:d],
        mixed_out[:, d:],
        small[2 : 2 + rank].T,
        slim[:rank],
        slim[rank],
        small[rank + 2, :HEAD_V],
        small[1],
        ffn_out[0],
        ffn_out[1],
        ffn_out[2],
    )


def solution(mesh):
    rows = P(("dp", "context"), None)
    grid = P(("dp", "context"), "tensor")
    placed = (
        (rows, rows, P("dp", "tensor", None, None), P())
        + (grid,) * 5
        + (P(), P(None, "tensor"), P("tensor"), P(), P())
        + (grid,) * 3
    )
    out = (
        (rows, rows, P())
        + (grid,) * 5
        + (P(), P(None, "tensor"), P("tensor"), P(), P())
        + (grid,) * 3
    )
    return jax.shard_map(local, mesh=mesh, in_specs=placed, out_specs=out, check_vma=False)
```
